256 devices in a mesh: rad: 8 (over y, x_hi), az: 32 (over z, x_lo, core).
Axes of the slice: x: 4 (x_hi: 2, x_lo: 2; x = x_hi * 2 + x_lo), y: 4, z: 8, core: 2. Of those that a mesh axis runs over, the one named last changes fastest.
Arguments:
- state: float32 [8, 8, 128, 4096], P(None, None, 'rad', 'az'), may hold values from -1.6 to 2, as said below
- shift: int32 [128], P('rad'), may hold values from 0 to 4095, as said below
Outputs:
- advanced: float32 [8, 8, 128, 4096], P(None, None, 'rad', 'az')
The draws below stay inside these ranges and needn't reach their ends.
Inputs may be any that keep to these rules, and one draw needn't show every extreme that they name: `state`: components: density (0) in 0.5 to 2, momentum (1 to 3) within 1.2 in magnitude, face fields (4 to 6) within 1.6 in magnitude, tracer (7) in 0 to 1. In each aligned block of the 16 rows of one device, at most 2 rows have the same value of shift // 128, and exactly 2 rows share one such value.
All inputs are finite; a program needn't handle non-finite values.
Results may differ from the reference program's by a relative error of at most 0.0003.
Values sent between devices are 32-bit elements; how exact they have to be, the bound alone decides.
A program may use at most 128 MiB of HBM per device.

```python
import jax
import jax.numpy as jnp
from jax import lax

R_DEV = 16
A_DEV = 128
Z = 8
NR = 128
NA = 4096
CAP = 2
N_RAD = 8
N_AZ = 32


def draw_state(key, part):
    keys = jax.random.split(key, 4)
    single = (1, Z, NR, NA)
    triple = (3, Z, NR, NA)
    density = jax.random.uniform(keys[0], single, jnp.float32, 0.5, 2.0)
    moment = 0.3 * jnp.clip(jax.random.normal(keys[1], triple, jnp.float32), -4.0, 4.0)
    faces = 0.4 * jnp.clip(jax.random.normal(keys[2], triple, jnp.float32), -4.0, 4.0)
    tracer = jax.random.uniform(keys[3], single, jnp.float32, 0.0, 1.0)
    return jnp.concatenate([density, moment, faces, tracer], axis=0).astype(jnp.float32)


def draw_shift(key, part):
    base_key = jax.random.fold_in(key, 7)
    block_total = NR // R_DEV
    spare_count = N_AZ * CAP - CAP - 1

    def one_block(block_index):
        subkeys = jax.random.split(jax.random.fold_in(base_key, block_index), 4)
        spare_slots = (CAP + 1 + jax.random.permutation(subkeys[0], spare_count)).astype(jnp.int32)
        chosen = jnp.concatenate([jnp.arange(CAP + 1, dtype=jnp.int32), spare_slots[:R_DEV - CAP - 1]])
        row_slots = jax.random.permutation(subkeys[1], chosen).astype(jnp.int32)
        shuffled = jax.random.permutation(subkeys[2], N_AZ).astype(jnp.int32)
        fixed_order = ((jnp.arange(N_AZ, dtype=jnp.int32) - 1) % N_AZ).astype(jnp.int32)
        offset_order = jnp.where(block_index == 0, fixed_order, shuffled)
        coarse = jnp.take(offset_order, row_slots // CAP)
        within = jax.random.randint(subkeys[3], (R_DEV,), 0, A_DEV, dtype=jnp.int32)
        first_block = block_index == 0
        within = jnp.where(first_block & (row_slots == 0), A_DEV - 1, jnp.where(first_block & (row_slots == CAP), 0, within))
        return (coarse * A_DEV + within).astype(jnp.int32)
    values = jax.vmap(one_block)(jnp.arange(block_total, dtype=jnp.int32))
    return values.reshape(NR).astype(jnp.int32)


def setup_inputs(seed: int = 0) -> dict:
    arg_keys = jax.random.split(jax.random.key(seed), 3)
    return {
        "state": draw_state(jax.random.fold_in(arg_keys[2], 71), 0),
        "shift": draw_shift(jax.random.fold_in(arg_keys[2], 71), 0),
    }


sound_sq = 1.0
time_step = 0.05
axis_of = (1, 2, 0)

def next_cell(values, direc):
    return jnp.roll(values, -1, axis_of[direc])

def prev_cell(values, direc):
    return jnp.roll(values, 1, axis_of[direc])

def physical(density, moment, center, tracer, normal, direc):
    velocity = [moment[k] / density for k in range(3)]
    fields = [normal if k == direc else center[k] for k in range(3)]
    square = fields[0] * fields[0] + fields[1] * fields[1] + fields[2] * fields[2]
    normal_speed = velocity[direc]
    mass_flux = moment[direc]
    moment_flux = [moment[k] * normal_speed - fields[k] * normal for k in range(3)]
    moment_flux[direc] = moment_flux[direc] + sound_sq * density + 0.5 * square
    induce = [normal_speed * fields[k] - velocity[k] * normal for k in range(3)]
    signal = jnp.abs(normal_speed) + jnp.sqrt(sound_sq + square / density)
    return (mass_flux, moment_flux, induce, tracer * normal_speed, signal)

def rusanov(density, moment, center, tracer, faces, direc):
    normal = faces[direc]
    left_density = prev_cell(density, direc)
    left_moment = [prev_cell(moment[k], direc) for k in range(3)]
    left_center = [prev_cell(center[k], direc) for k in range(3)]
    left_tracer = prev_cell(tracer, direc)
    left = physical(left_density, left_moment, left_center, left_tracer, normal, direc)
    right = physical(density, moment, center, tracer, normal, direc)
    signal = jnp.maximum(left[4], right[4])
    mass_flux = 0.5 * (left[0] + right[0]) - 0.5 * signal * (density - left_density)
    moment_flux = [0.5 * (left[1][k] + right[1][k]) - 0.5 * signal * (moment[k] - left_moment[k]) for k in range(3)]
    induce = [0.5 * (left[2][k] + right[2][k]) - 0.5 * signal * (center[k] - left_center[k]) for k in range(3)]
    tracer_flux = 0.5 * (left[3] + right[3]) - 0.5 * signal * (tracer - left_tracer)
    return (mass_flux, moment_flux, induce, tracer_flux)

def divergence(terms):
    total = next_cell(terms[0], 0) - terms[0]
    for direc in (1, 2):
        total = total + (next_cell(terms[direc], direc) - terms[direc])
    return total

def advance(block):
    density = block[0]
    moment = [block[1], block[2], block[3]]
    faces = [block[4], block[5], block[6]]
    tracer = block[7]
    center = [0.5 * (faces[k] + next_cell(faces[k], k)) for k in range(3)]
    fluxes = [rusanov(density, moment, center, tracer, faces, direc) for direc in range(3)]
    new_density = density - time_step * divergence([fluxes[d][0] for d in range(3)])
    new_moment = [moment[k] - time_step * divergence([fluxes[d][1][k] for d in range(3)]) for k in range(3)]
    new_tracer = tracer - time_step * divergence([fluxes[d][3] for d in range(3)])
    induce = [fluxes[d][2] for d in range(3)]
    edge_two = 0.25 * (induce[1][0] + prev_cell(induce[1][0], 0) - (induce[0][1] + prev_cell(induce[0][1], 1)))
    edge_zero = 0.25 * (induce[2][1] + prev_cell(induce[2][1], 1) - (induce[1][2] + prev_cell(induce[1][2], 2)))
    edge_one = 0.25 * (induce[0][2] + prev_cell(induce[0][2], 2) - (induce[2][0] + prev_cell(induce[2][0], 0)))
    face_zero = faces[0] - time_step * (next_cell(edge_two, 1) - edge_two - (next_cell(edge_one, 2) - edge_one))
    face_one = faces[1] - time_step * (next_cell(edge_zero, 2) - edge_zero - (next_cell(edge_two, 0) - edge_two))
    face_two = faces[2] - time_step * (next_cell(edge_one, 0) - edge_one - (next_cell(edge_zero, 1) - edge_zero))
    result = jnp.stack([new_density] + new_moment + [face_zero, face_one, face_two, new_tracer], axis=0)
    return result[:, :, 2:-2, 2:-2]

def reference(state, shift):

    def one_block(which):
        start = which * R_DEV
        rows = jnp.clip(start - 2 + jnp.arange(R_DEV + 4, dtype=jnp.int32), 0, NR - 1).astype(jnp.int32)
        block = jnp.take(state, rows, axis=2)
        row_shift = jnp.take(shift, rows).astype(jnp.int32)
        column = jnp.arange(NA, dtype=jnp.int32)
        source_col = ((column[None, :] - row_shift[:, None]) % NA).astype(jnp.int32)
        moved = jnp.take_along_axis(block, jnp.broadcast_to(source_col, block.shape), axis=3)
        wrapped = jnp.concatenate([moved[..., -2:], moved, moved[..., :2]], axis=3)
        return advance(wrapped)
    blocks = lax.map(one_block, jnp.arange(N_RAD, dtype=jnp.int32))
    return jnp.moveaxis(blocks, 0, 2).reshape(8, Z, NR, NA)
```

```python
import functools
import jax
import jax.numpy as jnp
from jax import lax
from jax.experimental import pallas as pl
from jax.experimental.pallas import tpu as pltpu
from jax.sharding import PartitionSpec as P

HALF_DT = 0.025
EDGE = 0.125


def turned(x, amount, axis):
    return pltpu.roll(x, amount % x.shape[axis], axis)


def cell_terms(w, c):
    rho, m0, m1, m2, _, _, _, tracer = w
    inv = 1.0 / rho
    v = [m0 * inv, m1 * inv, m2 * inv]
    m = [m0, m1, m2]
    sq = [c[0] * c[0], c[1] * c[1], c[2] * c[2]]
    return dict(rho=rho, m=m, c=c, s=tracer, inv=inv, v=v, sq=sq)


def side(t, d):
    j, k = [i for i in range(3) if i != d]
    vd = t["v"][d]
    return [
        t["rho"], t["m"][0], t["m"][1], t["m"][2], t["c"][j], t["c"][k], t["s"],
        t["inv"], t["v"][0], t["v"][1], t["v"][2], t["sq"][j] + t["sq"][k],
        t["m"][0] * vd, t["m"][1] * vd, t["m"][2] * vd,
        vd * t["c"][j], vd * t["c"][k], t["s"] * vd,
    ]


def face_flux(left, right, n, d):
    j, k = [i for i in range(3) if i != d]
    nn = n * n
    vl, vr = left[8 + d], right[8 + d]
    pl_, pr = nn + left[11], nn + right[11]
    signal = jnp.maximum(
        jnp.abs(vl) + jnp.sqrt(1.0 + pl_ * left[7]), jnp.abs(vr) + jnp.sqrt(1.0 + pr * right[7])
    )
    total = [left[i] + right[i] for i in range(18)]
    jump = [right[i] - left[i] for i in range(7)]
    mass = total[1 + d] - signal * jump[0]
    mom = [None] * 3
    mom[d] = total[12 + d] - 2.0 * nn + total[0] + 0.5 * (pl_ + pr) - signal * jump[1 + d]
    mom[j] = total[12 + j] - n * total[4] - signal * jump[1 + j]
    mom[k] = total[12 + k] - n * total[5] - signal * jump[1 + k]
    ind = [None] * 3
    ind[j] = total[15] - n * total[8 + j] - signal * jump[4]
    ind[k] = total[16] - n * total[8 + k] - signal * jump[5]
    tracer = total[17] - signal * jump[6]
    return [mass] + mom + [tracer], ind


def packed_advance(w, nxt, prv):
    b = w[4:7]
    c = [0.5 * (b[d] + nxt[d](b[d])) for d in range(3)]
    t = cell_terms(w, c)
    flow, ind = [], []
    for d in range(3):
        right = side(t, d)
        left = [prv[d](x) for x in right]
        f, g = face_flux(left, right, b[d], d)
        flow.append(f)
        ind.append(g)
    e2 = EDGE * (ind[1][0] + prv[0](ind[1][0]) - (ind[0][1] + prv[1](ind[0][1])))
    e0 = EDGE * (ind[2][1] + prv[1](ind[2][1]) - (ind[1][2] + prv[2](ind[1][2])))
    e1 = EDGE * (ind[0][2] + prv[2](ind[0][2]) - (ind[2][0] + prv[0](ind[2][0])))
    out = []
    for i, q in enumerate([w[0], w[1], w[2], w[3], w[7]]):
        div = nxt[0](flow[0][i]) - flow[0][i]
        for d in (1, 2):
            div = div + (nxt[d](flow[d][i]) - flow[d][i])
        out.append(q - HALF_DT * div)
    dt = 2.0 * HALF_DT
    f0 = b[0] - dt * (nxt[1](e2) - e2 - (nxt[2](e1) - e1))
    f1 = b[1] - dt * (nxt[2](e0) - e0 - (nxt[0](e2) - e2))
    f2 = b[2] - dt * (nxt[0](e1) - e1 - (nxt[1](e0) - e0))
    return [out[0], out[1], out[2], out[3], f0, f1, f2, out[4]]


def step_kernel(rows, rows_ref, low_ref, high_ref, out_ref, edge_ref):
    lane = lax.broadcasted_iota(jnp.int32, (8, 128), 1)
    sub = lane % 8
    nxt = [lambda x: turned(x, -8, 1), lambda x: turned(x, -1, 1), lambda x: turned(x, -1, 0)]
    prv = [lambda x: turned(x, 8, 1), lambda x: turned(x, 1, 1), lambda x: turned(x, 1, 0)]

    def fields(q, f):
        return rows_ref[q, f * 8:(f + 1) * 8, :]

    bases = [0, rows + 3 - 16]
    for tile, base in enumerate(bases):
        w = []
        for f in range(8):
            low, high = low_ref[f * 8:(f + 1) * 8, :], high_ref[f * 8:(f + 1) * 8, :]
            acc = jnp.ones((8, 128), jnp.float32)
            for g in range(16):
                q = base + g
                x = fields(q, f)
                here = lane // 8 == g
                a = jnp.where(sub < 4, turned(x, 8 * g + 1, 1), turned(x, 8 * g + 4 - 126, 1))
                a = jnp.where(sub == 0, turned(low, 8 * g - 2 * q - 1, 1), a)
                a = jnp.where(sub > 5, turned(high, 8 * g + 6 - 2 * q, 1), a)
                acc = jnp.where(here, a, acc)
            w.append(acc)
        for f, x in enumerate(packed_advance(w, nxt, prv)):
            edge_ref[tile, f * 8:(f + 1) * 8, :] = x

    az_n, az_p = nxt[1], prv[1]
    k_n, k_p = nxt[2], prv[2]

    def row_part(q):
        w = [fields(q, f) for f in range(8)]
        beyond = pltpu.roll(high_ref[40:48, :], lax.rem(127 - 2 * q + 128, 128), 1)
        after = jnp.where(lane == 127, beyond, az_n(w[5]))
        c = [0.5 * (w[4] + fields(q + 1, 4)), 0.5 * (w[5] + after), 0.5 * (w[6] + k_n(w[6]))]
        t = cell_terms(w, c)
        r1, r2 = side(t, 1), side(t, 2)
        flow1, ind1 = face_flux([az_p(x) for x in r1], r1, w[5], 1)
        flow2, ind2 = face_flux([k_p(x) for x in r2], r2, w[6], 2)
        return w, t, flow1, ind1, flow2, ind2

    def fresh(q):
        w, t, flow1, ind1, flow2, ind2 = row_part(q)
        return w, side(t, 0), flow1, ind1, flow2, ind2

    _, left, _, ind1, _, ind2 = fresh(jnp.int32(0))
    zero = jnp.zeros((8, 128), jnp.float32)
    start = tuple(left) + (ind1[0], ind2[0]) + (zero,) * 9

    def body(q, carry):
        left, p10, p20 = carry[:18], carry[18], carry[19]
        partial, part_b = carry[20:25], carry[25:28]
        pending_e2 = carry[28]
        w, right, flow1, ind1, flow2, ind2 = fresh(q)
        flow0, ind0 = face_flux(left, right, w[4], 0)
        e2 = EDGE * (ind1[0] + p10 - (ind0[1] + az_p(ind0[1])))
        e1 = EDGE * (ind0[2] + k_p(ind0[2]) - (ind2[0] + p20))
        e0 = EDGE * (ind2[1] + az_p(ind2[1]) - (ind1[2] + k_p(ind1[2])))
        dt = 2.0 * HALF_DT

        done = [partial[i] - HALF_DT * flow0[i] for i in range(5)]
        done_b = [part_b[0], part_b[1] + dt * e2, part_b[2] - dt * e1]
        fin = [done[0], done[1], done[2], done[3], done_b[0], done_b[1], done_b[2], done[4]]

        @pl.when(q >= 2)
        def _():
            r = q - 2
            second = (q - 1 >= 14).astype(jnp.int32)
            g = q - 1 - second * bases[1]
            for f in range(8):
                e = edge_ref[second, f * 8:(f + 1) * 8, :]
                val = jnp.where(lane == 0, pltpu.roll(e, lax.rem(128 + 127 - 8 * g, 128), 1), fin[f])
                val = jnp.where(lane == 127, pltpu.roll(e, lax.rem(128 + 122 - 8 * g, 128), 1), val)
                out_ref[pl.ds(f * 8 * rows + r, 8, stride=rows), :] = val

        new = []
        cells = [w[0], w[1], w[2], w[3], w[7]]
        for i in range(5):
            div = (az_n(flow1[i]) - flow1[i]) + (k_n(flow2[i]) - flow2[i]) - flow0[i]
            new.append(cells[i] - HALF_DT * div)
        n0 = w[4] - dt * (az_n(e2) - e2 - (k_n(e1) - e1))
        n1 = w[5] - dt * (k_n(e0) - e0 + e2)
        n2 = w[6] - dt * (-e1 - (az_n(e0) - e0))
        return tuple(right) + (ind1[0], ind2[0]) + tuple(new) + (n0, n1, n2, e2)

    lax.fori_loop(1, rows + 2, body, start)


def step(rows_form, low, high):
    q, _, width = rows_form.shape
    rows = q - 3
    out = pl.pallas_call(
        functools.partial(step_kernel, rows),
        out_shape=jax.ShapeDtypeStruct((64 * rows, width), jnp.float32),
        in_specs=[pl.BlockSpec(memory_space=pltpu.VMEM)] * 3,
        out_specs=pl.BlockSpec(memory_space=pltpu.VMEM),
        scratch_shapes=[pltpu.VMEM((2, 64, width), jnp.float32)],
        name="advance_rows",
    )(rows_form, low, high)
    return out.reshape(8, 8, rows, width)


def passed_along(value, axis, steps):
    count = lax.axis_size(axis)
    pairs = [(source, (source + steps) % count) for source in range(count)]
    return lax.ppermute(value, axis, pairs)


def with_halo(block, sides, width, periodic):
    for axis, dim in sides:
        count = lax.axis_size(axis)
        forward = [(i, i + 1) for i in range(count - 1)]
        if periodic:
            forward.append((count - 1, 0))
        backward = [(target, source) for source, target in forward]
        low = lax.ppermute(
            lax.slice_in_dim(block, block.shape[dim] - width, None, axis=dim), axis, forward
        )
        high = lax.ppermute(lax.slice_in_dim(block, 0, width, axis=dim), axis, backward)
        block = jnp.concatenate([low, block, high], axis=dim)
    return block


def outflow(padded, place, last_place):
    inner = padded[:, :, 2:-2]
    lower = jnp.where(
        place == 0, jnp.broadcast_to(inner[:, :, :1], padded[:, :, :2].shape), padded[:, :, :2]
    )
    upper = jnp.where(
        place == last_place,
        jnp.broadcast_to(inner[:, :, -1:], padded[:, :, -2:].shape),
        padded[:, :, -2:],
    )
    return jnp.concatenate([lower, inner, upper], axis=2)


def rotate_local(values, amount):
    row_width = values.shape[-1]
    last_axis = values.ndim - 1
    for bit_level in range((row_width - 1).bit_length()):
        rolled = jnp.roll(values, 1 << bit_level, axis=last_axis)
        chosen = amount // (1 << bit_level) % 2 == 1
        values = jnp.where(chosen[:, None], rolled, values)
    return values


def per_device(state, shift):
    row_count = state.shape[2]
    col_count = state.shape[3]
    column = lax.broadcasted_iota(jnp.int32, (row_count, col_count), 1)
    residual = shift % col_count
    coarse = shift // col_count
    rolled = rotate_local(state, residual)
    carried = passed_along(rolled, "az", 1)
    remapped = jnp.where((column >= residual[:, None])[None, None], rolled, carried)
    for bit_level in range((lax.axis_size("az") - 1).bit_length()):
        arrived = passed_along(remapped, "az", 1 << bit_level)
        chosen = coarse // (1 << bit_level) % 2 == 1
        remapped = jnp.where(chosen[None, None, :, None], arrived, remapped)
    place = lax.axis_index("rad")
    last_place = lax.axis_size("rad") - 1
    radial = with_halo(remapped, (("rad", 2),), 2, False)
    radial = outflow(radial, place, last_place)[:, :, 1:]
    rows_form = radial.transpose(2, 0, 1, 3).reshape(row_count + 3, 64, col_count)

    def edge(cells, steps):
        flat = cells.reshape(64, 2 * (row_count + 3))
        flat = jnp.pad(flat, ((0, 0), (0, col_count - flat.shape[1])))
        return passed_along(flat, "az", steps)

    low = edge(radial[..., -2:], 1)
    high = edge(radial[..., :2], -1)
    return step(rows_form, low, high)


def solution(mesh):
    placed = (P(None, None, "rad", "az"), P("rad"))
    return jax.shard_map(
        per_device,
        mesh=mesh,
        in_specs=placed,
        out_specs=P(None, None, "rad", "az"),
        check_vma=False,
    )
```

```python
import functools
import jax
import jax.numpy as jnp
from jax import lax
from jax.experimental import pallas as pl
from jax.experimental.pallas import tpu as pltpu
from jax.sharding import PartitionSpec as P

HALF_DT = 0.025
EDGE = 0.125


def turned(x, amount, axis):
    return pltpu.roll(x, amount % x.shape[axis], axis)


def cell_terms(w, c):
    rho, m0, m1, m2, _, _, _, tracer = w
    inv = 1.0 / rho
    v = [m0 * inv, m1 * inv, m2 * inv]
    m = [m0, m1, m2]
    sq = [c[0] * c[0], c[1] * c[1], c[2] * c[2]]
    return dict(rho=rho, m=m, c=c, s=tracer, inv=inv, v=v, sq=sq)


def side(t, d):
    j, k = [i for i in range(3) if i != d]
    vd = t["v"][d]
    return [
        t["rho"], t["m"][0], t["m"][1], t["m"][2], t["c"][j], t["c"][k], t["s"],
        t["inv"], t["v"][0], t["v"][1], t["v"][2], t["sq"][j] + t["sq"][k],
        t["m"][0] * vd, t["m"][1] * vd, t["m"][2] * vd,
        vd * t["c"][j], vd * t["c"][k], t["s"] * vd,
    ]


def face_flux(left, right, n, d):
    j, k = [i for i in range(3) if i != d]
    nn = n * n
    vl, vr = left[8 + d], right[8 + d]
    pl_, pr = nn + left[11], nn + right[11]
    signal = jnp.maximum(
        jnp.abs(vl) + jnp.sqrt(1.0 + pl_ * left[7]), jnp.abs(vr) + jnp.sqrt(1.0 + pr * right[7])
    )
    total = [left[i] + right[i] for i in range(18)]
    jump = [right[i] - left[i] for i in range(7)]
    mass = total[1 + d] - signal * jump[0]
    mom = [None] * 3
    mom[d] = total[12 + d] - 2.0 * nn + total[0] + 0.5 * (pl_ + pr) - signal * jump[1 + d]
    mom[j] = total[12 + j] - n * total[4] - signal * jump[1 + j]
    mom[k] = total[12 + k] - n * total[5] - signal * jump[1 + k]
    ind = [None] * 3
    ind[j] = total[15] - n * total[8 + j] - signal * jump[4]
    ind[k] = total[16] - n * total[8 + k] - signal * jump[5]
    tracer = total[17] - signal * jump[6]
    return [mass] + mom + [tracer], ind


def packed_advance(w, nxt, prv):
    b = w[4:7]
    c = [0.5 * (b[d] + nxt[d](b[d])) for d in range(3)]
    t = cell_terms(w, c)
    flow, ind = [], []
    for d in range(3):
        right = side(t, d)
        left = [prv[d](x) for x in right]
        f, g = face_flux(left, right, b[d], d)
        flow.append(f)
        ind.append(g)
    e2 = EDGE * (ind[1][0] + prv[0](ind[1][0]) - (ind[0][1] + prv[1](ind[0][1])))
    e0 = EDGE * (ind[2][1] + prv[1](ind[2][1]) - (ind[1][2] + prv[2](ind[1][2])))
    e1 = EDGE * (ind[0][2] + prv[2](ind[0][2]) - (ind[2][0] + prv[0](ind[2][0])))
    out = []
    for i, q in enumerate([w[0], w[1], w[2], w[3], w[7]]):
        div = nxt[0](flow[0][i]) - flow[0][i]
        for d in (1, 2):
            div = div + (nxt[d](flow[d][i]) - flow[d][i])
        out.append(q - HALF_DT * div)
    dt = 2.0 * HALF_DT
    f0 = b[0] - dt * (nxt[1](e2) - e2 - (nxt[2](e1) - e1))
    f1 = b[1] - dt * (nxt[2](e0) - e0 - (nxt[0](e2) - e2))
    f2 = b[2] - dt * (nxt[0](e1) - e1 - (nxt[1](e0) - e0))
    return [out[0], out[1], out[2], out[3], f0, f1, f2, out[4]]


def step_kernel(rows, rows_ref, low_ref, high_ref, out_ref, edge_ref):
    lane = lax.broadcasted_iota(jnp.int32, (8, 128), 1)
    sub = lane % 8
    nxt = [lambda x: turned(x, -8, 1), lambda x: turned(x, -1, 1), lambda x: turned(x, -1, 0)]
    prv = [lambda x: turned(x, 8, 1), lambda x: turned(x, 1, 1), lambda x: turned(x, 1, 0)]

    def fields(q, f):
        return rows_ref[q, f * 8:(f + 1) * 8, :]

    bases = [0, rows + 3 - 16]
    for tile, base in enumerate(bases):
        w = []
        for f in range(8):
            low, high = low_ref[f * 8:(f + 1) * 8, :], high_ref[f * 8:(f + 1) * 8, :]
            acc = jnp.ones((8, 128), jnp.float32)
            for g in range(16):
                q = base + g
                x = fields(q, f)
                here = lane // 8 == g
                a = jnp.where(sub < 4, turned(x, 8 * g + 1, 1), turned(x, 8 * g + 4 - 126, 1))
                a = jnp.where(sub == 0, turned(low, 8 * g - 2 * q - 1, 1), a)
                a = jnp.where(sub > 5, turned(high, 8 * g + 6 - 2 * q, 1), a)
                acc = jnp.where(here, a, acc)
            w.append(acc)
        for f, x in enumerate(packed_advance(w, nxt, prv)):
            edge_ref[tile, f * 8:(f + 1) * 8, :] = x

    az_n, az_p = nxt[1], prv[1]
    k_n, k_p = nxt[2], prv[2]

    def row_part(q):
        w = [fields(q, f) for f in range(8)]
        beyond = pltpu.roll(high_ref[40:48, :], lax.rem(127 - 2 * q + 128, 128), 1)
        after = jnp.where(lane == 127, beyond, az_n(w[5]))
        c = [0.5 * (w[4] + fields(q + 1, 4)), 0.5 * (w[5] + after), 0.5 * (w[6] + k_n(w[6]))]
        t = cell_terms(w, c)
        r1, r2 = side(t, 1), side(t, 2)
        flow1, ind1 = face_flux([az_p(x) for x in r1], r1, w[5], 1)
        flow2, ind2 = face_flux([k_p(x) for x in r2], r2, w[6], 2)
        return w, t, flow1, ind1, flow2, ind2

    def fresh(q):
        w, t, flow1, ind1, flow2, ind2 = row_part(q)
        return w, side(t, 0), flow1, ind1, flow2, ind2

    _, left, _, ind1, _, ind2 = fresh(jnp.int32(0))
    zero = jnp.zeros((8, 128), jnp.float32)
    start = tuple(left) + (ind1[0], ind2[0]) + (zero,) * 9

    def body(q, carry):
        left, p10, p20 = carry[:18], carry[18], carry[19]
        partial, part_b = carry[20:25], carry[25:28]
        pending_e2 = carry[28]
        w, right, flow1, ind1, flow2, ind2 = fresh(q)
        flow0, ind0 = face_flux(left, right, w[4], 0)
        e2 = EDGE * (ind1[0] + p10 - (ind0[1] + az_p(ind0[1])))
        e1 = EDGE * (ind0[2] + k_p(ind0[2]) - (ind2[0] + p20))
        e0 = EDGE * (ind2[1] + az_p(ind2[1]) - (ind1[2] + k_p(ind1[2])))
        dt = 2.0 * HALF_DT

        done = [partial[i] - HALF_DT * flow0[i] for i in range(5)]
        done_b = [part_b[0], part_b[1] + dt * e2, part_b[2] - dt * e1]
        fin = [done[0], done[1], done[2], done[3], done_b[0], done_b[1], done_b[2], done[4]]

        @pl.when(q >= 2)
        def _():
            r = q - 2
            second = (q - 1 >= 14).astype(jnp.int32)
            g = q - 1 - second * bases[1]
            for f in range(8):
                e = edge_ref[second, f * 8:(f + 1) * 8, :]
                val = jnp.where(lane == 0, pltpu.roll(e, lax.rem(128 + 127 - 8 * g, 128), 1), fin[f])
                val = jnp.where(lane == 127, pltpu.roll(e, lax.rem(128 + 122 - 8 * g, 128), 1), val)
                out_ref[pl.ds(f * 8 * rows + r, 8, stride=rows), :] = val

        new = []
        cells = [w[0], w[1], w[2], w[3], w[7]]
        for i in range(5):
            div = (az_n(flow1[i]) - flow1[i]) + (k_n(flow2[i]) - flow2[i]) - flow0[i]
            new.append(cells[i] - HALF_DT * div)
        n0 = w[4] - dt * (az_n(e2) - e2 - (k_n(e1) - e1))
        n1 = w[5] - dt * (k_n(e0) - e0 + e2)
        n2 = w[6] - dt * (-e1 - (az_n(e0) - e0))
        return tuple(right) + (ind1[0], ind2[0]) + tuple(new) + (n0, n1, n2, e2)

    lax.fori_loop(1, rows + 2, body, start)


def step(rows_form, low, high):
    q, _, width = rows_form.shape
    rows = q - 3
    out = pl.pallas_call(
        functools.partial(step_kernel, rows),
        out_shape=jax.ShapeDtypeStruct((64 * rows, width), jnp.float32),
        in_specs=[pl.BlockSpec(memory_space=pltpu.VMEM)] * 3,
        out_specs=pl.BlockSpec(memory_space=pltpu.VMEM),
        scratch_shapes=[pltpu.VMEM((2, 64, width), jnp.float32)],
        name="advance_rows",
    )(rows_form, low, high)
    return out.reshape(8, 8, rows, width)

MESH = pl.DeviceIdType.MESH
HOPS = 5
AHEAD, BACK = 5, 7
SLOTS = AHEAD + BACK
PARTS = 4


def plan_kernel(rows, rings, shift_ref, plan_ref):
    shape = (rows, 128)
    low = lax.axis_index("az") % 4
    down = lax.broadcasted_iota(jnp.int32, shape, 0)
    along = lax.broadcasted_iota(jnp.int32, shape, 1)
    amount = jnp.zeros(shape, jnp.int32)
    other = jnp.full(shape, -1, jnp.int32)
    for r in range(rows):
        amount = jnp.where(down == r, shift_ref[r], amount)
        other = jnp.where(along == r, shift_ref[r], other)
    coarse, other_coarse = amount // 128, other // 128
    chips = (low + coarse) // 4 % rings
    other_chips = (low + other_coarse) // 4 % rings
    real = along < rows
    key, other_key = chips * rows + down, other_chips * rows + along
    as_float = lambda x: x.astype(jnp.float32)
    before = as_float(jnp.where(real & (other_key < key), 1, 0))
    rank = jnp.sum(before, axis=1, keepdims=True)
    after = as_float(jnp.where(key < other_key, 1, 0))
    other_rank = jnp.sum(after, axis=0, keepdims=True)
    chips_f, other_chips_f = as_float(chips), as_float(other_chips)
    count = as_float(along)
    ahead = rank < count
    back_f = float(rings) - chips_f
    load_ahead = jnp.sum(jnp.where(ahead, chips_f, 0.0), axis=0, keepdims=True)
    load_back = jnp.sum(jnp.where(ahead, 0.0, back_f), axis=0, keepdims=True)
    far_ahead = jnp.max(jnp.where(ahead, chips_f, 0.0), axis=0, keepdims=True)
    far_back = jnp.max(jnp.where(ahead, 0.0, back_f), axis=0, keepdims=True)
    fits = (load_ahead <= AHEAD * HOPS) & (load_back <= BACK * HOPS) & (far_ahead <= HOPS) & (far_back <= HOPS)
    lanes_f = as_float(lax.broadcasted_iota(jnp.int32, (1, 128), 1))
    cut = jnp.min(jnp.where(fits & (lanes_f <= float(rows)), lanes_f, 128.0), axis=1, keepdims=True)
    back, other_back = rank >= cut, other_rank >= cut
    hops = jnp.where(back, back_f, chips_f)
    other_hops = jnp.where(other_back, float(rings) - other_chips_f, other_chips_f)
    side_f = jnp.where(back, 1.0, 0.0)
    other_side = jnp.where(other_back, 1.0, 0.0)
    first = jnp.sum(before * other_hops * jnp.where(side_f == other_side, 1.0, 0.0), axis=1, keepdims=True)
    hop = as_float(along)
    reach = first - hop + float(HOPS - 1)
    place = jnp.zeros(shape, jnp.float32)
    for k in range(1, max(AHEAD, BACK) + 1):
        place = place + jnp.where(reach >= float(HOPS * k), 1.0, 0.0)
    there = place * float(HOPS) + hop < first + hops
    arrival = jnp.where(there, place + side_f * float(AHEAD), -1.0)
    within = amount - coarse * 128
    turn = coarse % 4
    crosses = (low % 2 + turn) // 2 % 2
    table = jnp.where(along < HOPS, arrival.astype(jnp.int32), within)
    table = jnp.where(along == HOPS + 1, crosses, table)
    table = jnp.where(along == HOPS + 2, turn % 2, table)
    plan_ref[0:rows, :] = table
    slot = along % SLOTS
    slot_back = jnp.where(slot >= AHEAD, 1.0, 0.0)
    line = as_float(slot) - slot_back * float(AHEAD)
    line = line * float(HOPS) + as_float(along // SLOTS)
    inside = (side_f == slot_back) & (first <= line) & (line < first + hops)
    chosen = jnp.sum(jnp.where(inside, as_float(down), 0.0), axis=0, keepdims=True)
    plan_ref[rows:rows + 8, :] = jnp.broadcast_to(chosen, (8, 128)).astype(jnp.int32)


def travel_kernel(
    rows, n_az, n_rad, state_ref, plan_ref, out_ref, low_ref, high_ref,
    before_ref, cur_ref, pack_ref, come_ref, across_ref, twin_ref, under_ref, over_ref, edge_ref, edge_in_ref,
    send_sem, recv_sem,
):
    az, rad = lax.axis_index("az"), lax.axis_index("rad")
    low_bits = az % 4
    step_az = lambda k: {"az": (az + k + n_az) % n_az}
    next_az, prev_az, next_z, prev_z = step_az(1), step_az(-1), step_az(4), step_az(-4)
    across = {"az": az + 2 - 4 * (low_bits // 2)}
    twin = {"az": az + 1 - 2 * (az % 2)}
    above = {"rad": (rad + 1) % n_rad}
    below = {"rad": (rad + n_rad - 1) % n_rad}
    barrier = pltpu.get_barrier_semaphore()
    partners = [next_az, prev_az, next_z, prev_z, across, twin, above, below]
    for device in partners:
        pl.semaphore_signal(barrier, inc=1, device_id=device, device_id_type=MESH)
    pl.semaphore_wait(barrier, len(partners))

    fields = 8 // PARTS
    deep = fields * 8
    lane = lax.broadcasted_iota(jnp.int32, (8, 128), 1)
    count = [0]
    copies = {}

    def send(name, src, dst, device):
        copy = pltpu.make_async_remote_copy(
            src_ref=src, dst_ref=dst, send_sem=send_sem.at[count[0]], recv_sem=recv_sem.at[count[0]],
            device_id=device, device_id_type=MESH,
        )
        count[0] += 1
        copies[name] = copy
        copy.start()

    def each(n, width, fn):
        def some(i, _):
            for j in range(width):
                fn(i * width + j)
            return 0
        lax.fori_loop(0, n // width, some, 0)

    def depart(c, hop):
        def one(m):
            r = plan_ref[rows, hop * SLOTS + m]
            pack_ref[hop, c, m] = cur_ref[hop, c, r]
        each(SLOTS, 4, one)
        send(("ahead", c, hop), pack_ref.at[hop, c, 0:AHEAD], come_ref[hop * PARTS + c].at[0:AHEAD], next_z)
        send(("back", c, hop), pack_ref.at[hop, c, AHEAD:SLOTS], come_ref[hop * PARTS + c].at[AHEAD:SLOTS], prev_z)

    def merge(c, level, flag_lane, source):
        def one(r):
            flag = jnp.full((deep, 128), plan_ref[r, flag_lane], jnp.int32)
            cur_ref[level + 1, c, r] = jnp.where(flag == 1, source[c, r], cur_ref[level, c, r])
        each(rows, 4, one)

    def stage(k, c):
        if k == 0:
            part = pl.ds(c * fields * 8 * rows, fields * 8 * rows)
            send(("carry", c), state_ref.at[part], before_ref.at[part], next_az)
        elif k == 1:
            copies["carry", c].wait_recv()

            def one(r):
                amount = plan_ref[r, HOPS]
                bound = jnp.full((8, 128), 128 - amount, jnp.int32)
                for f in range(fields):
                    cells = pl.ds((c * fields + f) * 8 * rows + r, 8, stride=rows)
                    mixed = jnp.where(lane < bound, state_ref[cells, :], before_ref[cells, :])
                    cur_ref[0, c, r, f * 8:(f + 1) * 8, :] = pltpu.roll(mixed, amount, 1)
            each(rows, 4, one)
            depart(c, 0)
        elif k <= 1 + HOPS:
            hop = k - 2
            copies["ahead", c, hop].wait_recv()
            copies["back", c, hop].wait_recv()

            def one(r):
                slot = plan_ref[r, hop]
                come = come_ref[hop * PARTS + c][jnp.maximum(slot, 0)]
                flag = jnp.full((deep, 128), slot, jnp.int32)
                cur_ref[hop + 1, c, r] = jnp.where(flag >= 0, come, cur_ref[hop, c, r])
            each(rows, 4, one)
            if hop + 1 < HOPS:
                depart(c, hop + 1)
            else:
                send(("across", c), cur_ref.at[HOPS, c], across_ref.at[c], across)
        elif k == 2 + HOPS:
            copies["across", c].wait_recv()
            merge(c, HOPS, HOPS + 1, across_ref)
            send(("twin", c), cur_ref.at[HOPS + 1, c], twin_ref.at[c], twin)
        elif k == 3 + HOPS:
            copies["twin", c].wait_recv()
            merge(c, HOPS + 1, HOPS + 2, twin_ref)
            tall = 2 if c * fields <= 4 < (c + 1) * fields else 1
            final = cur_ref.at[HOPS + 2, c]
            send(("up", c), final.at[rows - 1:rows], under_ref.at[c], above)
            send(("down", c), final.at[0:tall], over_ref.at[c, 0:tall], below)

            def one(r):
                out_ref[r + 1, c * deep:(c + 1) * deep, :] = cur_ref[HOPS + 2, c, r]
            each(rows, 4, one)

    stages = 4 + HOPS
    for wave in range(stages + PARTS - 1):
        for c in range(PARTS):
            if 0 <= wave - c < stages:
                stage(wave - c, c)

    last = HOPS + 2

    def edges(f, get, first, n, low, high):
        for q in range(first, first + n):
            x = get(q)
            low = jnp.where(lane // 2 == q, pltpu.roll(x, (2 * q + 2) % 128, 1), low)
            high = jnp.where(lane // 2 == q, pltpu.roll(x, 2 * q, 1), high)
        return low, high

    for f in range(8):
        c, at = f // fields, (f % fields) * 8
        low = high = jnp.ones((8, 128), jnp.float32)
        low, high = edges(f, lambda q: cur_ref[last, c, q - 1, at:at + 8, :], 1, rows, low, high)
        edge_ref[0, f * 8:(f + 1) * 8, :] = low
        edge_ref[1, f * 8:(f + 1) * 8, :] = high
    at_start = jnp.full((8, 128), rad, jnp.int32) == 0
    at_end = jnp.full((8, 128), rad, jnp.int32) == n_rad - 1
    for c in range(PARTS):
        copies["up", c].wait_recv()
        copies["down", c].wait_recv()
        for f in range(fields):
            here = slice((c * fields + f) * 8, (c * fields + f + 1) * 8)
            at = slice(f * 8, f * 8 + 8)
            top = cur_ref[last, c, rows - 1, at, :]
            under = jnp.where(at_start, cur_ref[last, c, 0, at, :], under_ref[c, 0, at, :])
            over = jnp.where(at_end, top, over_ref[c, 0, at, :])
            beyond = top
            if c * fields + f == 4:
                beyond = jnp.where(at_end, top, over_ref[c, 1, at, :])
            out_ref[0, here, :] = under
            out_ref[rows + 1, here, :] = over
            out_ref[rows + 2, here, :] = beyond
            halo = {0: under, rows + 1: over, rows + 2: beyond}
            low, high = edge_ref[0, here, :], edge_ref[1, here, :]
            low, high = edges(f, lambda q: halo[q], 0, 1, low, high)
            low, high = edges(f, lambda q: halo[q], rows + 1, 2, low, high)
            edge_ref[2, here, :] = low
            edge_ref[3, here, :] = high
    send("low", edge_ref.at[2], edge_in_ref.at[0], next_az)
    send("high", edge_ref.at[3], edge_in_ref.at[1], prev_az)
    copies["low"].wait_recv()
    low_ref[...] = edge_in_ref[0]
    copies["high"].wait_recv()
    high_ref[...] = edge_in_ref[1]
    for copy in copies.values():
        copy.wait_send()


def travel(state, shift, n_az, n_rad):
    rows, width = state.shape[2], state.shape[3]
    plan = pl.pallas_call(
        functools.partial(plan_kernel, rows, n_az // 4),
        out_shape=jax.ShapeDtypeStruct((rows + 8, 128), jnp.int32),
        in_specs=[pl.BlockSpec(memory_space=pltpu.SMEM)],
        out_specs=pl.BlockSpec(memory_space=pltpu.VMEM),
        name="plan_routes",
    )(shift)
    deep = 64 // PARTS
    f32 = jnp.float32
    vmem = pl.BlockSpec(memory_space=pltpu.VMEM)
    n_copies = PARTS * (5 + 2 * HOPS) + 2
    return pl.pallas_call(
        functools.partial(travel_kernel, rows, n_az, n_rad),
        out_shape=[
            jax.ShapeDtypeStruct((rows + 3, 64, width), f32),
            jax.ShapeDtypeStruct((64, width), f32),
            jax.ShapeDtypeStruct((64, width), f32),
        ],
        in_specs=[vmem, pl.BlockSpec(memory_space=pltpu.SMEM)],
        out_specs=[vmem] * 3,
        scratch_shapes=[
            pltpu.VMEM((64 * rows, width), f32),
            pltpu.VMEM((HOPS + 3, PARTS, rows, deep, width), f32),
            pltpu.VMEM((HOPS, PARTS, SLOTS, deep, width), f32),
            [pltpu.VMEM((SLOTS, deep, width), f32)] * (HOPS * PARTS),
            pltpu.VMEM((PARTS, rows, deep, width), f32),
            pltpu.VMEM((PARTS, rows, deep, width), f32),
            pltpu.VMEM((PARTS, 1, deep, width), f32),
            pltpu.VMEM((PARTS, 2, deep, width), f32),
            pltpu.VMEM((4, 64, width), f32),
            pltpu.VMEM((2, 64, width), f32),
            pltpu.SemaphoreType.DMA((n_copies,)),
            pltpu.SemaphoreType.DMA((n_copies,)),
        ],
        compiler_params=pltpu.CompilerParams(collective_id=0, has_side_effects=True),
        name="travel_rows",
    )(state.reshape(64 * rows, width), plan)


def solution(mesh):
    n_az, n_rad = mesh.shape["az"], mesh.shape["rad"]

    def per_device(state, shift):
        rows_form, low, high = travel(state, shift, n_az, n_rad)
        return step(rows_form, low, high)

    return jax.shard_map(
        per_device,
        mesh=mesh,
        in_specs=(P(None, None, "rad", "az"), P("rad")),
        out_specs=P(None, None, "rad", "az"),
        check_vma=False,
    )
```

```python
import functools
import jax
import jax.numpy as jnp
from jax import lax
from jax.experimental import pallas as pl
from jax.experimental.pallas import tpu as pltpu
from jax.sharding import PartitionSpec as P

HALF_DT = 0.025
EDGE = 0.125


def turned(x, amount, axis):
    return pltpu.roll(x, amount % x.shape[axis], axis)


def cell_terms(w, c):
    rho, m0, m1, m2, _, _, _, tracer = w
    inv = 1.0 / rho
    v = [m0 * inv, m1 * inv, m2 * inv]
    m = [m0, m1, m2]
    sq = [c[0] * c[0], c[1] * c[1], c[2] * c[2]]
    return dict(rho=rho, m=m, c=c, s=tracer, inv=inv, v=v, sq=sq)


def side(t, d):
    j, k = [i for i in range(3) if i != d]
    vd = t["v"][d]
    return [
        t["rho"], t["m"][0], t["m"][1], t["m"][2], t["c"][j], t["c"][k], t["s"],
        t["inv"], t["v"][0], t["v"][1], t["v"][2], t["sq"][j] + t["sq"][k],
        t["m"][0] * vd, t["m"][1] * vd, t["m"][2] * vd,
        vd * t["c"][j], vd * t["c"][k], t["s"] * vd,
    ]


def face_flux(left, right, n, d):
    j, k = [i for i in range(3) if i != d]
    nn = n * n
    vl, vr = left[8 + d], right[8 + d]
    pl_, pr = nn + left[11], nn + right[11]
    signal = jnp.maximum(
        jnp.abs(vl) + jnp.sqrt(1.0 + pl_ * left[7]), jnp.abs(vr) + jnp.sqrt(1.0 + pr * right[7])
    )
    total = [left[i] + right[i] for i in range(18)]
    jump = [right[i] - left[i] for i in range(7)]
    mass = total[1 + d] - signal * jump[0]
    mom = [None] * 3
    mom[d] = total[12 + d] - 2.0 * nn + total[0] + 0.5 * (pl_ + pr) - signal * jump[1 + d]
    mom[j] = total[12 + j] - n * total[4] - signal * jump[1 + j]
    mom[k] = total[12 + k] - n * total[5] - signal * jump[1 + k]
    ind = [None] * 3
    ind[j] = total[15] - n * total[8 + j] - signal * jump[4]
    ind[k] = total[16] - n * total[8 + k] - signal * jump[5]
    tracer = total[17] - signal * jump[6]
    return [mass] + mom + [tracer], ind


def packed_advance(w, nxt, prv):
    b = w[4:7]
    c = [0.5 * (b[d] + nxt[d](b[d])) for d in range(3)]
    t = cell_terms(w, c)
    flow, ind = [], []
    for d in range(3):
        right = side(t, d)
        left = [prv[d](x) for x in right]
        f, g = face_flux(left, right, b[d], d)
        flow.append(f)
        ind.append(g)
    e2 = EDGE * (ind[1][0] + prv[0](ind[1][0]) - (ind[0][1] + prv[1](ind[0][1])))
    e0 = EDGE * (ind[2][1] + prv[1](ind[2][1]) - (ind[1][2] + prv[2](ind[1][2])))
    e1 = EDGE * (ind[0][2] + prv[2](ind[0][2]) - (ind[2][0] + prv[0](ind[2][0])))
    out = []
    for i, q in enumerate([w[0], w[1], w[2], w[3], w[7]]):
        div = nxt[0](flow[0][i]) - flow[0][i]
        for d in (1, 2):
            div = div + (nxt[d](flow[d][i]) - flow[d][i])
        out.append(q - HALF_DT * div)
    dt = 2.0 * HALF_DT
    f0 = b[0] - dt * (nxt[1](e2) - e2 - (nxt[2](e1) - e1))
    f1 = b[1] - dt * (nxt[2](e0) - e0 - (nxt[0](e2) - e2))
    f2 = b[2] - dt * (nxt[0](e1) - e1 - (nxt[1](e0) - e0))
    return [out[0], out[1], out[2], out[3], f0, f1, f2, out[4]]


def step_kernel(rows, rows_ref, low_ref, high_ref, out_ref, edge_ref):
    lane = lax.broadcasted_iota(jnp.int32, (8, 128), 1)
    sub = lane % 8
    nxt = [lambda x: turned(x, -8, 1), lambda x: turned(x, -1, 1), lambda x: turned(x, -1, 0)]
    prv = [lambda x: turned(x, 8, 1), lambda x: turned(x, 1, 1), lambda x: turned(x, 1, 0)]

    def fields(q, f):
        return rows_ref[q, f * 8:(f + 1) * 8, :]

    bases = [0, rows + 3 - 16]
    for tile, base in enumerate(bases):
        w = []
        for f in range(8):
            low, high = low_ref[f * 8:(f + 1) * 8, :], high_ref[f * 8:(f + 1) * 8, :]
            acc = jnp.ones((8, 128), jnp.float32)
            for g in range(16):
                q = base + g
                x = fields(q, f)
                here = lane // 8 == g
                a = jnp.where(sub < 4, turned(x, 8 * g + 1, 1), turned(x, 8 * g + 4 - 126, 1))
                a = jnp.where(sub == 0, turned(low, 8 * g - 2 * q - 1, 1), a)
                a = jnp.where(sub > 5, turned(high, 8 * g + 6 - 2 * q, 1), a)
                acc = jnp.where(here, a, acc)
            w.append(acc)
        for f, x in enumerate(packed_advance(w, nxt, prv)):
            edge_ref[tile, f * 8:(f + 1) * 8, :] = x

    az_n, az_p = nxt[1], prv[1]
    k_n, k_p = nxt[2], prv[2]

    def row_part(q):
        w = [fields(q, f) for f in range(8)]
        beyond = pltpu.roll(high_ref[40:48, :], lax.rem(127 - 2 * q + 128, 128), 1)
        after = jnp.where(lane == 127, beyond, az_n(w[5]))
        c = [0.5 * (w[4] + fields(q + 1, 4)), 0.5 * (w[5] + after), 0.5 * (w[6] + k_n(w[6]))]
        t = cell_terms(w, c)
        r1, r2 = side(t, 1), side(t, 2)
        flow1, ind1 = face_flux([az_p(x) for x in r1], r1, w[5], 1)
        flow2, ind2 = face_flux([k_p(x) for x in r2], r2, w[6], 2)
        return w, t, flow1, ind1, flow2, ind2

    def fresh(q):
        w, t, flow1, ind1, flow2, ind2 = row_part(q)
        return w, side(t, 0), flow1, ind1, flow2, ind2

    _, left, _, ind1, _, ind2 = fresh(jnp.int32(0))
    zero = jnp.zeros((8, 128), jnp.float32)
    start = tuple(left) + (ind1[0], ind2[0]) + (zero,) * 9

    def body(q, carry):
        left, p10, p20 = carry[:18], carry[18], carry[19]
        partial, part_b = carry[20:25], carry[25:28]
        pending_e2 = carry[28]
        w, right, flow1, ind1, flow2, ind2 = fresh(q)
        flow0, ind0 = face_flux(left, right, w[4], 0)
        e2 = EDGE * (ind1[0] + p10 - (ind0[1] + az_p(ind0[1])))
        e1 = EDGE * (ind0[2] + k_p(ind0[2]) - (ind2[0] + p20))
        e0 = EDGE * (ind2[1] + az_p(ind2[1]) - (ind1[2] + k_p(ind1[2])))
        dt = 2.0 * HALF_DT

        done = [partial[i] - HALF_DT * flow0[i] for i in range(5)]
        done_b = [part_b[0], part_b[1] + dt * e2, part_b[2] - dt * e1]
        fin = [done[0], done[1], done[2], done[3], done_b[0], done_b[1], done_b[2], done[4]]

        @pl.when(q >= 2)
        def _():
            r = q - 2
            second = (q - 1 >= 14).astype(jnp.int32)
            g = q - 1 - second * bases[1]
            for f in range(8):
                e = edge_ref[second, f * 8:(f + 1) * 8, :]
                val = jnp.where(lane == 0, pltpu.roll(e, lax.rem(128 + 127 - 8 * g, 128), 1), fin[f])
                val = jnp.where(lane == 127, pltpu.roll(e, lax.rem(128 + 122 - 8 * g, 128), 1), val)
                out_ref[pl.ds(f * 8 * rows + r, 8, stride=rows), :] = val

        new = []
        cells = [w[0], w[1], w[2], w[3], w[7]]
        for i in range(5):
            div = (az_n(flow1[i]) - flow1[i]) + (k_n(flow2[i]) - flow2[i]) - flow0[i]
            new.append(cells[i] - HALF_DT * div)
        n0 = w[4] - dt * (az_n(e2) - e2 - (k_n(e1) - e1))
        n1 = w[5] - dt * (k_n(e0) - e0 + e2)
        n2 = w[6] - dt * (-e1 - (az_n(e0) - e0))
        return tuple(right) + (ind1[0], ind2[0]) + tuple(new) + (n0, n1, n2, e2)

    lax.fori_loop(1, rows + 2, body, start)


def step(rows_form, low, high):
    q, _, width = rows_form.shape
    rows = q - 3
    out = pl.pallas_call(
        functools.partial(step_kernel, rows),
        out_shape=jax.ShapeDtypeStruct((64 * rows, width), jnp.float32),
        in_specs=[pl.BlockSpec(memory_space=pltpu.VMEM)] * 3,
        out_specs=pl.BlockSpec(memory_space=pltpu.VMEM),
        scratch_shapes=[pltpu.VMEM((2, 64, width), jnp.float32)],
        name="advance_rows",
    )(rows_form, low, high)
    return out.reshape(8, 8, rows, width)

MESH = pl.DeviceIdType.MESH
HOPS = 5
AHEAD, BACK = 5, 7
SLOTS = AHEAD + BACK
PARTS = 4


def plan_kernel(rows, rings, shift_ref, plan_ref):
    shape = (rows, 128)
    low = lax.axis_index("az") % 4
    down = lax.broadcasted_iota(jnp.int32, shape, 0)
    along = lax.broadcasted_iota(jnp.int32, shape, 1)
    amount = jnp.zeros(shape, jnp.int32)
    other = jnp.full(shape, -1, jnp.int32)
    for r in range(rows):
        amount = jnp.where(down == r, shift_ref[r], amount)
        other = jnp.where(along == r, shift_ref[r], other)
    coarse, other_coarse = amount // 128, other // 128
    chips = (low + coarse) // 4 % rings
    other_chips = (low + other_coarse) // 4 % rings
    real = along < rows
    key, other_key = chips * rows + down, other_chips * rows + along
    as_float = lambda x: x.astype(jnp.float32)
    before = as_float(jnp.where(real & (other_key < key), 1, 0))
    rank = jnp.sum(before, axis=1, keepdims=True)
    after = as_float(jnp.where(key < other_key, 1, 0))
    other_rank = jnp.sum(after, axis=0, keepdims=True)
    chips_f, other_chips_f = as_float(chips), as_float(other_chips)
    count = as_float(along)
    ahead = rank < count
    back_f = float(rings) - chips_f
    load_ahead = jnp.sum(jnp.where(ahead, chips_f, 0.0), axis=0, keepdims=True)
    load_back = jnp.sum(jnp.where(ahead, 0.0, back_f), axis=0, keepdims=True)
    far_ahead = jnp.max(jnp.where(ahead, chips_f, 0.0), axis=0, keepdims=True)
    far_back = jnp.max(jnp.where(ahead, 0.0, back_f), axis=0, keepdims=True)
    fits = (load_ahead <= AHEAD * HOPS) & (load_back <= BACK * HOPS) & (far_ahead <= HOPS) & (far_back <= HOPS)
    lanes_f = as_float(lax.broadcasted_iota(jnp.int32, (1, 128), 1))
    cut = jnp.min(jnp.where(fits & (lanes_f <= float(rows)), lanes_f, 128.0), axis=1, keepdims=True)
    back, other_back = rank >= cut, other_rank >= cut
    hops = jnp.where(back, back_f, chips_f)
    other_hops = jnp.where(other_back, float(rings) - other_chips_f, other_chips_f)
    side_f = jnp.where(back, 1.0, 0.0)
    other_side = jnp.where(other_back, 1.0, 0.0)
    first = jnp.sum(before * other_hops * jnp.where(side_f == other_side, 1.0, 0.0), axis=1, keepdims=True)
    hop = as_float(along)
    reach = first - hop + float(HOPS - 1)
    place = jnp.zeros(shape, jnp.float32)
    for k in range(1, max(AHEAD, BACK) + 1):
        place = place + jnp.where(reach >= float(HOPS * k), 1.0, 0.0)
    there = place * float(HOPS) + hop < first + hops
    arrival = jnp.where(there, place + side_f * float(AHEAD), -1.0)
    within = amount - coarse * 128
    turn = coarse % 4
    crosses = (low % 2 + turn) // 2 % 2
    table = jnp.where(along < HOPS, arrival.astype(jnp.int32), within)
    table = jnp.where(along == HOPS + 1, crosses, table)
    table = jnp.where(along == HOPS + 2, turn % 2, table)
    plan_ref[0:rows, :] = table
    slot = along % SLOTS
    slot_back = jnp.where(slot >= AHEAD, 1.0, 0.0)
    line = as_float(slot) - slot_back * float(AHEAD)
    line = line * float(HOPS) + as_float(along // SLOTS)
    inside = (side_f == slot_back) & (first <= line) & (line < first + hops)
    chosen = jnp.sum(jnp.where(inside, as_float(down), 0.0), axis=0, keepdims=True)
    plan_ref[rows:rows + 8, :] = jnp.broadcast_to(chosen, (8, 128)).astype(jnp.int32)


def travel_kernel(
    rows, n_az, n_rad, state_ref, plan_ref, out_ref, low_ref, high_ref,
    before_ref, cur_ref, pack_ref, come_ref, across_ref, twin_ref, under_ref, over_ref, edge_ref, edge_in_ref,
    send_sem, recv_sem,
):
    az, rad = lax.axis_index("az"), lax.axis_index("rad")
    low_bits = az % 4
    step_az = lambda k: {"az": (az + k + n_az) % n_az}
    next_az, prev_az, next_z, prev_z = step_az(1), step_az(-1), step_az(4), step_az(-4)
    across = {"az": az + 2 - 4 * (low_bits // 2)}
    twin = {"az": az + 1 - 2 * (az % 2)}
    above = {"rad": (rad + 1) % n_rad}
    below = {"rad": (rad + n_rad - 1) % n_rad}
    barrier = pltpu.get_barrier_semaphore()
    partners = [next_az, prev_az, next_z, prev_z, across, twin, above, below]
    for device in partners:
        pl.semaphore_signal(barrier, inc=1, device_id=device, device_id_type=MESH)
    pl.semaphore_wait(barrier, len(partners))

    fields = 8 // PARTS
    deep = fields * 8
    lane = lax.broadcasted_iota(jnp.int32, (8, 128), 1)
    count = [0]
    copies = {}

    def send(name, src, dst, device):
        copy = pltpu.make_async_remote_copy(
            src_ref=src, dst_ref=dst, send_sem=send_sem.at[count[0]], recv_sem=recv_sem.at[count[0]],
            device_id=device, device_id_type=MESH,
        )
        count[0] += 1
        copies[name] = copy
        copy.start()

    def each(n, width, fn):
        def some(i, _):
            for j in range(width):
                fn(i * width + j)
            return 0
        lax.fori_loop(0, n // width, some, 0)

    def depart(c, hop):
        def one(m):
            r = plan_ref[rows, hop * SLOTS + m]
            pack_ref[hop, c, m] = cur_ref[hop, c, r]
        each(SLOTS, 4, one)
        send(("ahead", c, hop), pack_ref.at[hop, c, 0:AHEAD], come_ref[hop * PARTS + c].at[0:AHEAD], next_z)
        send(("back", c, hop), pack_ref.at[hop, c, AHEAD:SLOTS], come_ref[hop * PARTS + c].at[AHEAD:SLOTS], prev_z)

    def merge(c, level, flag_lane, source):
        def one(r):
            flag = jnp.full((deep, 128), plan_ref[r, flag_lane], jnp.int32)
            cur_ref[level + 1, c, r] = jnp.where(flag == 1, source[c, r], cur_ref[level, c, r])
        each(rows, 4, one)

    def stage(k, c):
        if k == 0:
            part = pl.ds(c * fields * 8 * rows, fields * 8 * rows)
            send(("carry", c), state_ref.at[part], before_ref.at[part], next_az)
        elif k == 1:
            copies["carry", c].wait_recv()

            def one(r):
                amount = plan_ref[r, HOPS]
                bound = jnp.full((8, 128), 128 - amount, jnp.int32)
                for f in range(fields):
                    cells = pl.ds((c * fields + f) * 8 * rows + r, 8, stride=rows)
                    mixed = jnp.where(lane < bound, state_ref[cells, :], before_ref[cells, :])
                    cur_ref[0, c, r, f * 8:(f + 1) * 8, :] = pltpu.roll(mixed, amount, 1)
            each(rows, 4, one)
            depart(c, 0)
        elif k <= 1 + HOPS:
            hop = k - 2
            copies["ahead", c, hop].wait_recv()
            copies["back", c, hop].wait_recv()

            def one(r):
                slot = plan_ref[r, hop]
                come = come_ref[hop * PARTS + c][jnp.maximum(slot, 0)]
                flag = jnp.full((deep, 128), slot, jnp.int32)
                cur_ref[hop + 1, c, r] = jnp.where(flag >= 0, come, cur_ref[hop, c, r])
            each(rows, 4, one)
            if hop + 1 < HOPS:
                depart(c, hop + 1)
            else:
                send(("across", c), cur_ref.at[HOPS, c], across_ref.at[c], across)
        elif k == 2 + HOPS:
            copies["across", c].wait_recv()
            merge(c, HOPS, HOPS + 1, across_ref)
            send(("twin", c), cur_ref.at[HOPS + 1, c], twin_ref.at[c], twin)
        elif k == 3 + HOPS:
            copies["twin", c].wait_recv()
            merge(c, HOPS + 1, HOPS + 2, twin_ref)
            tall = 2 if c * fields <= 4 < (c + 1) * fields else 1
            final = cur_ref.at[HOPS + 2, c]
            send(("up", c), final.at[rows - 1:rows], under_ref.at[c], above)
            send(("down", c), final.at[0:tall], over_ref.at[c, 0:tall], below)

            def one(r):
                out_ref[r + 1, c * deep:(c + 1) * deep, :] = cur_ref[HOPS + 2, c, r]
            each(rows, 4, one)
            for f in range(fields):
                here = slice((c * fields + f) * 8, (c * fields + f + 1) * 8)
                at = slice(f * 8, f * 8 + 8)
                low = high = jnp.ones((8, 128), jnp.float32)
                low, high = edges(lambda q: cur_ref[last, c, q - 1, at, :], 1, rows, low, high)
                edge_ref[0, here, :] = low
                edge_ref[1, here, :] = high
        elif k == 4 + HOPS:
            copies["up", c].wait_recv()
            copies["down", c].wait_recv()
            for f in range(fields):
                here = slice((c * fields + f) * 8, (c * fields + f + 1) * 8)
                at = slice(f * 8, f * 8 + 8)
                top = cur_ref[last, c, rows - 1, at, :]
                under = jnp.where(at_start, cur_ref[last, c, 0, at, :], under_ref[c, 0, at, :])
                over = jnp.where(at_end, top, over_ref[c, 0, at, :])
                beyond = top
                if c * fields + f == 4:
                    beyond = jnp.where(at_end, top, over_ref[c, 1, at, :])
                out_ref[0, here, :] = under
                out_ref[rows + 1, here, :] = over
                out_ref[rows + 2, here, :] = beyond
                halo = {0: under, rows + 1: over, rows + 2: beyond}
                low, high = edge_ref[0, here, :], edge_ref[1, here, :]
                low, high = edges(lambda q: halo[q], 0, 1, low, high)
                low, high = edges(lambda q: halo[q], rows + 1, 2, low, high)
                edge_ref[2, here, :] = low
                edge_ref[3, here, :] = high
            part = slice(c * deep, (c + 1) * deep)
            send(("low", c), edge_ref.at[2, part], edge_in_ref.at[0, part], next_az)
            send(("high", c), edge_ref.at[3, part], edge_in_ref.at[1, part], prev_az)
        elif k == 5 + HOPS:
            part = slice(c * deep, (c + 1) * deep)
            copies["low", c].wait_recv()
            low_ref[part, :] = edge_in_ref[0, part, :]
            copies["high", c].wait_recv()
            high_ref[part, :] = edge_in_ref[1, part, :]

    last = HOPS + 2
    at_start = jnp.full((8, 128), rad, jnp.int32) == 0
    at_end = jnp.full((8, 128), rad, jnp.int32) == n_rad - 1

    def edges(get, first, n, low, high):
        for q in range(first, first + n):
            x = get(q)
            low = jnp.where(lane // 2 == q, pltpu.roll(x, (2 * q + 2) % 128, 1), low)
            high = jnp.where(lane // 2 == q, pltpu.roll(x, 2 * q, 1), high)
        return low, high

    for c in range(PARTS):
        stage(0, c)
    stages = 6 + HOPS
    for wave in range(1, stages + PARTS - 1):
        for c in range(PARTS):
            if 1 <= wave - c < stages:
                stage(wave - c, c)

    for copy in copies.values():
        copy.wait_send()


def travel(state, shift, n_az, n_rad):
    rows, width = state.shape[2], state.shape[3]
    plan = pl.pallas_call(
        functools.partial(plan_kernel, rows, n_az // 4),
        out_shape=jax.ShapeDtypeStruct((rows + 8, 128), jnp.int32),
        in_specs=[pl.BlockSpec(memory_space=pltpu.SMEM)],
        out_specs=pl.BlockSpec(memory_space=pltpu.VMEM),
        name="plan_routes",
    )(shift)
    deep = 64 // PARTS
    f32 = jnp.float32
    vmem = pl.BlockSpec(memory_space=pltpu.VMEM)
    n_copies = PARTS * (7 + 2 * HOPS)
    return pl.pallas_call(
        functools.partial(travel_kernel, rows, n_az, n_rad),
        out_shape=[
            jax.ShapeDtypeStruct((rows + 3, 64, width), f32),
            jax.ShapeDtypeStruct((64, width), f32),
            jax.ShapeDtypeStruct((64, width), f32),
        ],
        in_specs=[vmem, pl.BlockSpec(memory_space=pltpu.SMEM)],
        out_specs=[vmem] * 3,
        scratch_shapes=[
            pltpu.VMEM((64 * rows, width), f32),
            pltpu.VMEM((HOPS + 3, PARTS, rows, deep, width), f32),
            pltpu.VMEM((HOPS, PARTS, SLOTS, deep, width), f32),
            [pltpu.VMEM((SLOTS, deep, width), f32)] * (HOPS * PARTS),
            pltpu.VMEM((PARTS, rows, deep, width), f32),
            pltpu.VMEM((PARTS, rows, deep, width), f32),
            pltpu.VMEM((PARTS, 1, deep, width), f32),
            pltpu.VMEM((PARTS, 2, deep, width), f32),
            pltpu.VMEM((4, 64, width), f32),
            pltpu.VMEM((2, 64, width), f32),
            pltpu.SemaphoreType.DMA((n_copies,)),
            pltpu.SemaphoreType.DMA((n_copies,)),
        ],
        compiler_params=pltpu.CompilerParams(collective_id=0, has_side_effects=True),
        name="travel_rows",
    )(state.reshape(64 * rows, width), plan)


def solution(mesh):
    n_az, n_rad = mesh.shape["az"], mesh.shape["rad"]

    def per_device(state, shift):
        rows_form, low, high = travel(state, shift, n_az, n_rad)
        return step(rows_form, low, high)

    return jax.shard_map(
        per_device,
        mesh=mesh,
        in_specs=(P(None, None, "rad", "az"), P("rad")),
        out_specs=P(None, None, "rad", "az"),
        check_vma=False,
    )
```

```python
import functools
import jax
import jax.numpy as jnp
from jax import lax
from jax.experimental import pallas as pl
from jax.experimental.pallas import tpu as pltpu
from jax.sharding import PartitionSpec as P

HALF_DT = 0.025
EDGE = 0.125


def turned(x, amount, axis):
    return pltpu.roll(x, amount % x.shape[axis], axis)


def cell_terms(w, c):
    rho, m0, m1, m2, _, _, _, tracer = w
    inv = 1.0 / rho
    v = [m0 * inv, m1 * inv, m2 * inv]
    m = [m0, m1, m2]
    sq = [c[0] * c[0], c[1] * c[1], c[2] * c[2]]
    return dict(rho=rho, m=m, c=c, s=tracer, inv=inv, v=v, sq=sq)


def side(t, d):
    j, k = [i for i in range(3) if i != d]
    vd = t["v"][d]
    return [
        t["rho"], t["m"][0], t["m"][1], t["m"][2], t["c"][j], t["c"][k], t["s"],
        t["inv"], t["v"][0], t["v"][1], t["v"][2], t["sq"][j] + t["sq"][k],
        t["m"][0] * vd, t["m"][1] * vd, t["m"][2] * vd,
        vd * t["c"][j], vd * t["c"][k], t["s"] * vd,
    ]


def face_flux(left, right, n, d):
    j, k = [i for i in range(3) if i != d]
    nn = n * n
    vl, vr = left[8 + d], right[8 + d]
    pl_, pr = nn + left[11], nn + right[11]
    signal = jnp.maximum(
        jnp.abs(vl) + jnp.sqrt(1.0 + pl_ * left[7]), jnp.abs(vr) + jnp.sqrt(1.0 + pr * right[7])
    )
    total = [left[i] + right[i] for i in range(18)]
    jump = [right[i] - left[i] for i in range(7)]
    mass = total[1 + d] - signal * jump[0]
    mom = [None] * 3
    mom[d] = total[12 + d] - 2.0 * nn + total[0] + 0.5 * (pl_ + pr) - signal * jump[1 + d]
    mom[j] = total[12 + j] - n * total[4] - signal * jump[1 + j]
    mom[k] = total[12 + k] - n * total[5] - signal * jump[1 + k]
    ind = [None] * 3
    ind[j] = total[15] - n * total[8 + j] - signal * jump[4]
    ind[k] = total[16] - n * total[8 + k] - signal * jump[5]
    tracer = total[17] - signal * jump[6]
    return [mass] + mom + [tracer], ind


def packed_advance(w, nxt, prv):
    b = w[4:7]
    c = [0.5 * (b[d] + nxt[d](b[d])) for d in range(3)]
    t = cell_terms(w, c)
    flow, ind = [], []
    for d in range(3):
        right = side(t, d)
        left = [prv[d](x) for x in right]
        f, g = face_flux(left, right, b[d], d)
        flow.append(f)
        ind.append(g)
    e2 = EDGE * (ind[1][0] + prv[0](ind[1][0]) - (ind[0][1] + prv[1](ind[0][1])))
    e0 = EDGE * (ind[2][1] + prv[1](ind[2][1]) - (ind[1][2] + prv[2](ind[1][2])))
    e1 = EDGE * (ind[0][2] + prv[2](ind[0][2]) - (ind[2][0] + prv[0](ind[2][0])))
    out = []
    for i, q in enumerate([w[0], w[1], w[2], w[3], w[7]]):
        div = nxt[0](flow[0][i]) - flow[0][i]
        for d in (1, 2):
            div = div + (nxt[d](flow[d][i]) - flow[d][i])
        out.append(q - HALF_DT * div)
    dt = 2.0 * HALF_DT
    f0 = b[0] - dt * (nxt[1](e2) - e2 - (nxt[2](e1) - e1))
    f1 = b[1] - dt * (nxt[2](e0) - e0 - (nxt[0](e2) - e2))
    f2 = b[2] - dt * (nxt[0](e1) - e1 - (nxt[1](e0) - e0))
    return [out[0], out[1], out[2], out[3], f0, f1, f2, out[4]]


def step_kernel(rows, rows_ref, low_ref, high_ref, out_ref, edge_ref):
    lane = lax.broadcasted_iota(jnp.int32, (8, 128), 1)
    sub = lane % 8
    nxt = [lambda x: turned(x, -8, 1), lambda x: turned(x, -1, 1), lambda x: turned(x, -1, 0)]
    prv = [lambda x: turned(x, 8, 1), lambda x: turned(x, 1, 1), lambda x: turned(x, 1, 0)]

    def fields(q, f):
        return rows_ref[q, f * 8:(f + 1) * 8, :]

    bases = [0, rows + 3 - 16]
    for tile, base in enumerate(bases):
        w = []
        for f in range(8):
            low, high = low_ref[f * 8:(f + 1) * 8, :], high_ref[f * 8:(f + 1) * 8, :]
            acc = jnp.ones((8, 128), jnp.float32)
            for g in range(16):
                q = base + g
                x = fields(q, f)
                here = lane // 8 == g
                a = jnp.where(sub < 4, turned(x, 8 * g + 1, 1), turned(x, 8 * g + 4 - 126, 1))
                a = jnp.where(sub == 0, turned(low, 8 * g - 2 * q - 1, 1), a)
                a = jnp.where(sub > 5, turned(high, 8 * g + 6 - 2 * q, 1), a)
                acc = jnp.where(here, a, acc)
            w.append(acc)
        for f, x in enumerate(packed_advance(w, nxt, prv)):
            edge_ref[tile, f * 8:(f + 1) * 8, :] = x

    az_n, az_p = nxt[1], prv[1]
    k_n, k_p = nxt[2], prv[2]

    def row_part(q):
        w = [fields(q, f) for f in range(8)]
        beyond = pltpu.roll(high_ref[40:48, :], lax.rem(127 - 2 * q + 128, 128), 1)
        after = jnp.where(lane == 127, beyond, az_n(w[5]))
        c = [0.5 * (w[4] + fields(q + 1, 4)), 0.5 * (w[5] + after), 0.5 * (w[6] + k_n(w[6]))]
        t = cell_terms(w, c)
        r1, r2 = side(t, 1), side(t, 2)
        flow1, ind1 = face_flux([az_p(x) for x in r1], r1, w[5], 1)
        flow2, ind2 = face_flux([k_p(x) for x in r2], r2, w[6], 2)
        return w, t, flow1, ind1, flow2, ind2

    def fresh(q):
        w, t, flow1, ind1, flow2, ind2 = row_part(q)
        return w, side(t, 0), flow1, ind1, flow2, ind2

    _, left, _, ind1, _, ind2 = fresh(jnp.int32(0))
    zero = jnp.zeros((8, 128), jnp.float32)
    start = tuple(left) + (ind1[0], ind2[0]) + (zero,) * 9

    def body(q, carry):
        left, p10, p20 = carry[:18], carry[18], carry[19]
        partial, part_b = carry[20:25], carry[25:28]
        pending_e2 = carry[28]
        w, right, flow1, ind1, flow2, ind2 = fresh(q)
        flow0, ind0 = face_flux(left, right, w[4], 0)
        e2 = EDGE * (ind1[0] + p10 - (ind0[1] + az_p(ind0[1])))
        e1 = EDGE * (ind0[2] + k_p(ind0[2]) - (ind2[0] + p20))
        e0 = EDGE * (ind2[1] + az_p(ind2[1]) - (ind1[2] + k_p(ind1[2])))
        dt = 2.0 * HALF_DT

        done = [partial[i] - HALF_DT * flow0[i] for i in range(5)]
        done_b = [part_b[0], part_b[1] + dt * e2, part_b[2] - dt * e1]
        fin = [done[0], done[1], done[2], done[3], done_b[0], done_b[1], done_b[2], done[4]]

        @pl.when(q >= 2)
        def _():
            r = q - 2
            second = (q - 1 >= 14).astype(jnp.int32)
            g = q - 1 - second * bases[1]
            for f in range(8):
                e = edge_ref[second, f * 8:(f + 1) * 8, :]
                val = jnp.where(lane == 0, pltpu.roll(e, lax.rem(128 + 127 - 8 * g, 128), 1), fin[f])
                val = jnp.where(lane == 127, pltpu.roll(e, lax.rem(128 + 122 - 8 * g, 128), 1), val)
                out_ref[pl.ds(f * 8 * rows + r, 8, stride=rows), :] = val

        new = []
        cells = [w[0], w[1], w[2], w[3], w[7]]
        for i in range(5):
            div = (az_n(flow1[i]) - flow1[i]) + (k_n(flow2[i]) - flow2[i]) - flow0[i]
            new.append(cells[i] - HALF_DT * div)
        n0 = w[4] - dt * (az_n(e2) - e2 - (k_n(e1) - e1))
        n1 = w[5] - dt * (k_n(e0) - e0 + e2)
        n2 = w[6] - dt * (-e1 - (az_n(e0) - e0))
        return tuple(right) + (ind1[0], ind2[0]) + tuple(new) + (n0, n1, n2, e2)

    lax.fori_loop(1, rows + 2, body, start)


def step(rows_form, low, high):
    q, _, width = rows_form.shape
    rows = q - 3
    out = pl.pallas_call(
        functools.partial(step_kernel, rows),
        out_shape=jax.ShapeDtypeStruct((64 * rows, width), jnp.float32),
        in_specs=[pl.BlockSpec(memory_space=pltpu.VMEM)] * 3,
        out_specs=pl.BlockSpec(memory_space=pltpu.VMEM),
        scratch_shapes=[pltpu.VMEM((2, 64, width), jnp.float32)],
        name="advance_rows",
    )(rows_form, low, high)
    return out.reshape(8, 8, rows, width)

MESH = pl.DeviceIdType.MESH
HOPS = 5
AHEAD, BACK = 5, 7
SLOTS = AHEAD + BACK
PARTS = 4


def plan_kernel(rows, rings, shift_ref, plan_ref):
    shape = (rows, 128)
    low = lax.axis_index("az") % 4
    down = lax.broadcasted_iota(jnp.int32, shape, 0)
    along = lax.broadcasted_iota(jnp.int32, shape, 1)
    amount = jnp.zeros(shape, jnp.int32)
    other = jnp.full(shape, -1, jnp.int32)
    for r in range(rows):
        amount = jnp.where(down == r, shift_ref[r], amount)
        other = jnp.where(along == r, shift_ref[r], other)
    coarse, other_coarse = amount // 128, other // 128
    chips = (low + coarse) // 4 % rings
    other_chips = (low + other_coarse) // 4 % rings
    real = along < rows
    key, other_key = chips * rows + down, other_chips * rows + along
    as_float = lambda x: x.astype(jnp.float32)
    before = as_float(jnp.where(real & (other_key < key), 1, 0))
    rank = jnp.sum(before, axis=1, keepdims=True)
    after = as_float(jnp.where(key < other_key, 1, 0))
    other_rank = jnp.sum(after, axis=0, keepdims=True)
    chips_f, other_chips_f = as_float(chips), as_float(other_chips)
    count = as_float(along)
    ahead = rank < count
    back_f = float(rings) - chips_f
    load_ahead = jnp.sum(jnp.where(ahead, chips_f, 0.0), axis=0, keepdims=True)
    load_back = jnp.sum(jnp.where(ahead, 0.0, back_f), axis=0, keepdims=True)
    far_ahead = jnp.max(jnp.where(ahead, chips_f, 0.0), axis=0, keepdims=True)
    far_back = jnp.max(jnp.where(ahead, 0.0, back_f), axis=0, keepdims=True)
    fits = (load_ahead <= AHEAD * HOPS) & (load_back <= BACK * HOPS) & (far_ahead <= HOPS) & (far_back <= HOPS)
    lanes_f = as_float(lax.broadcasted_iota(jnp.int32, (1, 128), 1))
    cut = jnp.min(jnp.where(fits & (lanes_f <= float(rows)), lanes_f, 128.0), axis=1, keepdims=True)
    back, other_back = rank >= cut, other_rank >= cut
    hops = jnp.where(back, back_f, chips_f)
    other_hops = jnp.where(other_back, float(rings) - other_chips_f, other_chips_f)
    side_f = jnp.where(back, 1.0, 0.0)
    other_side = jnp.where(other_back, 1.0, 0.0)
    first = jnp.sum(before * other_hops * jnp.where(side_f == other_side, 1.0, 0.0), axis=1, keepdims=True)
    hop = as_float(along)
    reach = first - hop + float(HOPS - 1)
    place = jnp.zeros(shape, jnp.float32)
    for k in range(1, max(AHEAD, BACK) + 1):
        place = place + jnp.where(reach >= float(HOPS * k), 1.0, 0.0)
    there = place * float(HOPS) + hop < first + hops
    arrival = jnp.where(there, place + side_f * float(AHEAD), -1.0)
    within = amount - coarse * 128
    turn = coarse % 4
    crosses = (low % 2 + turn) // 2 % 2
    table = jnp.where(along < HOPS, arrival.astype(jnp.int32), within)
    table = jnp.where(along == HOPS + 1, crosses, table)
    table = jnp.where(along == HOPS + 2, turn % 2, table)
    plan_ref[0:rows, :] = table
    slot = along % SLOTS
    slot_back = jnp.where(slot >= AHEAD, 1.0, 0.0)
    line = as_float(slot) - slot_back * float(AHEAD)
    line = line * float(HOPS) + as_float(along // SLOTS)
    inside = (side_f == slot_back) & (first <= line) & (line < first + hops)
    chosen = jnp.sum(jnp.where(inside, as_float(down), 0.0), axis=0, keepdims=True)
    plan_ref[rows:rows + 8, :] = jnp.broadcast_to(chosen, (8, 128)).astype(jnp.int32)


def travel_kernel(
    rows, n_az, n_rad, state_ref, plan_ref, out_ref, low_ref, high_ref,
    before_ref, cur_ref, pack_ref, come_ref, across_ref, twin_ref, under_ref, over_ref, edge_ref, edge_in_ref,
    send_sem, recv_sem,
):
    az, rad = lax.axis_index("az"), lax.axis_index("rad")
    low_bits = az % 4
    step_az = lambda k: {"az": (az + k + n_az) % n_az}
    next_az, prev_az, next_z, prev_z = step_az(1), step_az(-1), step_az(4), step_az(-4)
    across = {"az": az + 2 - 4 * (low_bits // 2)}
    twin = {"az": az + 1 - 2 * (az % 2)}
    above = {"rad": (rad + 1) % n_rad}
    below = {"rad": (rad + n_rad - 1) % n_rad}
    barrier = pltpu.get_barrier_semaphore()
    partners = [next_az, prev_az, next_z, prev_z, across, twin, above, below]
    for device in partners:
        pl.semaphore_signal(barrier, inc=1, device_id=device, device_id_type=MESH)
    pl.semaphore_wait(barrier, len(partners))

    fields = 8 // PARTS
    deep = fields * 8
    lane = lax.broadcasted_iota(jnp.int32, (8, 128), 1)
    count = [0]
    copies = {}

    def send(name, src, dst, device):
        copy = pltpu.make_async_remote_copy(
            src_ref=src, dst_ref=dst, send_sem=send_sem.at[count[0]], recv_sem=recv_sem.at[count[0]],
            device_id=device, device_id_type=MESH,
        )
        count[0] += 1
        copies[name] = copy
        copy.start()

    def each(n, load, store):
        values = [load(i) for i in range(n)]
        for i in range(n):
            store(i, values[i])

    def depart(c, hop):
        def put(m, x):
            pack_ref[hop, c, m] = x
        each(SLOTS, lambda m: cur_ref[hop, c, plan_ref[rows, hop * SLOTS + m]], put)
        send(("ahead", c, hop), pack_ref.at[hop, c, 0:AHEAD], come_ref[hop * PARTS + c].at[0:AHEAD], next_z)
        send(("back", c, hop), pack_ref.at[hop, c, AHEAD:SLOTS], come_ref[hop * PARTS + c].at[AHEAD:SLOTS], prev_z)

    def merge(c, level, flag_lane, source):
        def one(r):
            flag = jnp.full((deep, 128), plan_ref[r, flag_lane], jnp.int32)
            return jnp.where(flag == 1, source[c, r], cur_ref[level, c, r])

        def put(r, x):
            cur_ref[level + 1, c, r] = x
        each(rows, one, put)

    def stage(k, c):
        if k == 0:
            part = pl.ds(c * fields * 8 * rows, fields * 8 * rows)
            send(("carry", c), state_ref.at[part], before_ref.at[part], next_az)
        elif k == 1:
            copies["carry", c].wait_recv()

            def one(r):
                amount = plan_ref[r, HOPS]
                bound = jnp.full((8, 128), 128 - amount, jnp.int32)
                found = []
                for f in range(fields):
                    cells = pl.ds((c * fields + f) * 8 * rows + r, 8, stride=rows)
                    mixed = jnp.where(lane < bound, state_ref[cells, :], before_ref[cells, :])
                    found.append(pltpu.roll(mixed, amount, 1))
                return found

            def put(r, found):
                for f in range(fields):
                    cur_ref[0, c, r, f * 8:(f + 1) * 8, :] = found[f]
            each(rows, one, put)
            depart(c, 0)
        elif k <= 1 + HOPS:
            hop = k - 2
            copies["ahead", c, hop].wait_recv()
            copies["back", c, hop].wait_recv()

            def one(r):
                slot = plan_ref[r, hop]
                come = come_ref[hop * PARTS + c][jnp.maximum(slot, 0)]
                flag = jnp.full((deep, 128), slot, jnp.int32)
                return jnp.where(flag >= 0, come, cur_ref[hop, c, r])

            def put(r, x):
                cur_ref[hop + 1, c, r] = x
            each(rows, one, put)
            if hop + 1 < HOPS:
                depart(c, hop + 1)
            else:
                send(("across", c), cur_ref.at[HOPS, c], across_ref.at[c], across)
        elif k == 2 + HOPS:
            copies["across", c].wait_recv()
            merge(c, HOPS, HOPS + 1, across_ref)
            send(("twin", c), cur_ref.at[HOPS + 1, c], twin_ref.at[c], twin)
        elif k == 3 + HOPS:
            copies["twin", c].wait_recv()
            merge(c, HOPS + 1, HOPS + 2, twin_ref)
            tall = 2 if c * fields <= 4 < (c + 1) * fields else 1
            final = cur_ref.at[HOPS + 2, c]
            send(("up", c), final.at[rows - 1:rows], under_ref.at[c], above)
            send(("down", c), final.at[0:tall], over_ref.at[c, 0:tall], below)

            def put(r, x):
                out_ref[r + 1, c * deep:(c + 1) * deep, :] = x
            each(rows, lambda r: cur_ref[HOPS + 2, c, r], put)

    stages = 4 + HOPS
    for wave in range(stages + PARTS - 1):
        for c in range(PARTS):
            if 0 <= wave - c < stages:
                stage(wave - c, c)

    last = HOPS + 2

    def edges(f, get, first, n, low, high):
        for q in range(first, first + n):
            x = get(q)
            low = jnp.where(lane // 2 == q, pltpu.roll(x, (2 * q + 2) % 128, 1), low)
            high = jnp.where(lane // 2 == q, pltpu.roll(x, 2 * q, 1), high)
        return low, high

    for f in range(8):
        c, at = f // fields, (f % fields) * 8
        low = high = jnp.ones((8, 128), jnp.float32)
        low, high = edges(f, lambda q: cur_ref[last, c, q - 1, at:at + 8, :], 1, rows, low, high)
        edge_ref[0, f * 8:(f + 1) * 8, :] = low
        edge_ref[1, f * 8:(f + 1) * 8, :] = high
    at_start = jnp.full((8, 128), rad, jnp.int32) == 0
    at_end = jnp.full((8, 128), rad, jnp.int32) == n_rad - 1
    for c in range(PARTS):
        copies["up", c].wait_recv()
        copies["down", c].wait_recv()
        for f in range(fields):
            here = slice((c * fields + f) * 8, (c * fields + f + 1) * 8)
            at = slice(f * 8, f * 8 + 8)
            top = cur_ref[last, c, rows - 1, at, :]
            under = jnp.where(at_start, cur_ref[last, c, 0, at, :], under_ref[c, 0, at, :])
            over = jnp.where(at_end, top, over_ref[c, 0, at, :])
            beyond = top
            if c * fields + f == 4:
                beyond = jnp.where(at_end, top, over_ref[c, 1, at, :])
            out_ref[0, here, :] = under
            out_ref[rows + 1, here, :] = over
            out_ref[rows + 2, here, :] = beyond
            halo = {0: under, rows + 1: over, rows + 2: beyond}
            low, high = edge_ref[0, here, :], edge_ref[1, here, :]
            low, high = edges(f, lambda q: halo[q], 0, 1, low, high)
            low, high = edges(f, lambda q: halo[q], rows + 1, 2, low, high)
            edge_ref[2, here, :] = low
            edge_ref[3, here, :] = high
    send("low", edge_ref.at[2], edge_in_ref.at[0], next_az)
    send("high", edge_ref.at[3], edge_in_ref.at[1], prev_az)
    copies["low"].wait_recv()
    low_ref[...] = edge_in_ref[0]
    copies["high"].wait_recv()
    high_ref[...] = edge_in_ref[1]
    for copy in copies.values():
        copy.wait_send()


def travel(state, shift, n_az, n_rad):
    rows, width = state.shape[2], state.shape[3]
    plan = pl.pallas_call(
        functools.partial(plan_kernel, rows, n_az // 4),
        out_shape=jax.ShapeDtypeStruct((rows + 8, 128), jnp.int32),
        in_specs=[pl.BlockSpec(memory_space=pltpu.SMEM)],
        out_specs=pl.BlockSpec(memory_space=pltpu.VMEM),
        name="plan_routes",
    )(shift)
    deep = 64 // PARTS
    f32 = jnp.float32
    vmem = pl.BlockSpec(memory_space=pltpu.VMEM)
    n_copies = PARTS * (5 + 2 * HOPS) + 2
    return pl.pallas_call(
        functools.partial(travel_kernel, rows, n_az, n_rad),
        out_shape=[
            jax.ShapeDtypeStruct((rows + 3, 64, width), f32),
            jax.ShapeDtypeStruct((64, width), f32),
            jax.ShapeDtypeStruct((64, width), f32),
        ],
        in_specs=[vmem, pl.BlockSpec(memory_space=pltpu.SMEM)],
        out_specs=[vmem] * 3,
        scratch_shapes=[
            pltpu.VMEM((64 * rows, width), f32),
            pltpu.VMEM((HOPS + 3, PARTS, rows, deep, width), f32),
            pltpu.VMEM((HOPS, PARTS, SLOTS, deep, width), f32),
            [pltpu.VMEM((SLOTS, deep, width), f32)] * (HOPS * PARTS),
            pltpu.VMEM((PARTS, rows, deep, width), f32),
            pltpu.VMEM((PARTS, rows, deep, width), f32),
            pltpu.VMEM((PARTS, 1, deep, width), f32),
            pltpu.VMEM((PARTS, 2, deep, width), f32),
            pltpu.VMEM((4, 64, width), f32),
            pltpu.VMEM((2, 64, width), f32),
            pltpu.SemaphoreType.DMA((n_copies,)),
            pltpu.SemaphoreType.DMA((n_copies,)),
        ],
        compiler_params=pltpu.CompilerParams(collective_id=0, has_side_effects=True),
        name="travel_rows",
    )(state.reshape(64 * rows, width), plan)


def solution(mesh):
    n_az, n_rad = mesh.shape["az"], mesh.shape["rad"]

    def per_device(state, shift):
        rows_form, low, high = travel(state, shift, n_az, n_rad)
        return step(rows_form, low, high)

    return jax.shard_map(
        per_device,
        mesh=mesh,
        in_specs=(P(None, None, "rad", "az"), P("rad")),
        out_specs=P(None, None, "rad", "az"),
        check_vma=False,
    )
```
